32 devices in a mesh: slab: 4 (over y, x), tile: 8 (over z, core).
Axes of the slice: x: 2, y: 2, z: 4, core: 2. Of those that a mesh axis runs over, the one named last changes fastest.
Arguments:
- state: float32 [256, 128, 1024], P('slab', 'tile'), may hold values from -6 to 6
- coeff: float32 [256, 128, 1024], P('slab', 'tile'), may hold values from 0.04 to 0.16
- target: float32 [256, 128, 1024], P('slab', 'tile'), may hold values from -6 to 6
- control: float32 [4, 128, 1024], P('slab', 'tile'), may hold values from -6 to 6
- multiplier: float32 [4, 128, 1024], P('slab', 'tile'), may hold values from -6 to 6
Outputs:
- final_state: float32 [256, 128, 1024], P('slab', 'tile')
- adjoint_start: float32 [256, 128, 1024], P('slab', 'tile')
- new_control: float32 [4, 128, 1024], P('slab', 'tile')
- new_multiplier: float32 [4, 128, 1024], P('slab', 'tile')
The draws below stay inside these ranges and needn't reach their ends.
All inputs are finite; a program needn't handle non-finite values.
Results may differ from the reference program's by a relative error of at most 0.00002.
Values sent between devices are 32-bit elements; how exact they have to be, the bound alone decides.
No kernel may reach another device: no remote copies, remote signals or barrier semaphores. Data moves between devices by JAX's collectives and lax.ppermute only.
A program may use at most 128 MiB of HBM per device.

```python
import jax
import jax.numpy as jnp

CZ = 64
NY = 1024
NZ = 256
NX = 128
N_SLAB = 4


def levels(own_key, dims, cuts, least, high):
    level = 1.0
    for dim, parts in cuts:
        steps = jax.random.uniform(jax.random.fold_in(jax.random.fold_in(own_key, 6), dim), (parts,), jnp.float32, least / len(cuts), high / len(cuts))
        level = level * jnp.repeat(jnp.exp(steps), dims[dim] // parts).reshape((-1,) + (1,) * (len(dims) - 1 - dim))
    return level


def centred(key, shape, spread, most, pieces=(), dtype=jnp.bfloat16):
    gain = levels(key, shape, pieces, -0.22, 0.18) if pieces else 1.0
    values = jax.random.normal(key, shape, jnp.float32) * spread * gain
    return jnp.minimum(jnp.maximum(values, -most), most).astype(dtype)


def setup_inputs(seed: int = 0) -> dict:
    splits = jax.random.split(jax.random.key(seed), 6)
    state = centred(splits[0], (NZ, NX, NY), 1.0, 6.0, ((0, 4), (1, 8)), jnp.float32)
    coeff = jnp.clip(0.04 + 0.12 * jax.random.uniform(splits[1], (NZ, NX, NY), jnp.float32) ** levels(splits[1], (NZ, NX, NY), ((0, 4), (1, 8)), -0.2, 0.2), 0.04, 0.16)
    target = centred(splits[2], (NZ, NX, NY), 1.0, 6.0, ((0, 4), (1, 8)), jnp.float32)
    control = centred(splits[3], (N_SLAB, NX, NY), 1.0, 6.0, ((0, 4), (1, 8)), jnp.float32)
    multiplier = centred(splits[4], (N_SLAB, NX, NY), 1.0, 6.0, ((0, 4), (1, 8)), jnp.float32)
    return dict(state=state, coeff=coeff, target=target, control=control, multiplier=multiplier)


rho_step = 0.5
tau_step = 0.5


def ghost_lap(field, below_plane, above_plane):
    blocks = field.reshape(N_SLAB, CZ, NX, NY)
    upper = jnp.concatenate([blocks[:, 1:], above_plane[:, None]], axis=1).reshape(NZ, NX, NY)
    lower = jnp.concatenate([below_plane[:, None], blocks[:, :-1]], axis=1).reshape(NZ, NX, NY)
    padded = jnp.pad(field, ((0, 0), (1, 1), (1, 1)))
    beside = padded[:, 2:, 1:-1] + padded[:, :-2, 1:-1] + padded[:, 1:-1, 2:] + padded[:, 1:-1, :-2]
    return upper + lower + beside - 6.0 * field


def reference(state, coeff, target, control, multiplier):
    below_plane = jnp.roll(control, 1, axis=0)
    zero_plane = jnp.zeros_like(control)
    middle = state + coeff * ghost_lap(state, below_plane, control)
    final_state = middle + coeff * ghost_lap(middle, below_plane, control)
    adj_two = final_state - target
    adj_one = adj_two + ghost_lap(coeff * adj_two, zero_plane, zero_plane)
    adjoint_start = adj_one + ghost_lap(coeff * adj_one, zero_plane, zero_plane)
    fin_blocks = final_state.reshape(N_SLAB, CZ, NX, NY)
    flux = (coeff * (adj_one + adj_two)).reshape(N_SLAB, CZ, NX, NY)
    upper_trace = fin_blocks[:, -1]
    lower_trace = jnp.roll(fin_blocks[:, 0], -1, axis=0)
    grad = flux[:, -1] + jnp.roll(flux[:, 0], -1, axis=0)
    new_multiplier = multiplier + rho_step * (upper_trace - lower_trace)
    new_control = (control - tau_step * (grad + new_multiplier)) / (1.0 + tau_step)
    return final_state, adjoint_start, new_control, new_multiplier
```

```python
from functools import partial

import jax
import jax.numpy as jnp
from jax import lax
from jax.experimental import pallas as pl
from jax.experimental.pallas import tpu as pltpu
from jax.sharding import PartitionSpec as P

rho_step = 0.5
tau_step = 0.5
f32 = jnp.float32
LANES = 128
SUB = 8
U = 8
MIB = 1 << 20


def copy(src, dst, sem):
    return pltpu.make_async_copy(src, dst, sem)


def nat(x):
    z, r, y = x.shape
    x = x.reshape(z, r // SUB, SUB, y // LANES, LANES).transpose(0, 1, 3, 2, 4)
    return x.reshape(z * r * y // LANES, LANES)


def unnat(x, shape):
    z, r, y = shape
    x = x.reshape(z, r // SUB, y // LANES, SUB, LANES).transpose(0, 1, 3, 2, 4)
    return x.reshape(shape)


def row_at(base, x, J):
    return pl.ds(base + (x // SUB) * (SUB * J) + x % SUB, J, stride=SUB)


def lane_masks(J):
    lane = lax.broadcasted_iota(jnp.int32, (J, LANES), 1)
    return lane == 0, lane == LANES - 1


def beside(ref, at, centre, J, masks):
    first, last = masks
    up = pltpu.roll(jnp.where(first, ref[pl.ds(at + 1, J), :], centre), LANES - 1, 1)
    down = pltpu.roll(jnp.where(last, ref[pl.ds(at - 1, J), :], centre), 1, 1)
    return up + down


def clear_pads(ref, lines, J):
    zero = jnp.zeros((J, LANES), f32)

    def body(i, _):
        for q in range(8):
            ref[pl.ds(pl.multiple_of(i * 16 * J, 16 * J) + q * 2 * J, J), :] = zero
        return 0

    lax.fori_loop(0, lines // 8, body, 0)
    ref[pl.ds(lines * 2 * J, J), :] = zero


class Lines(dict):
    def __init__(self, load):
        self.load = load

    def __missing__(self, x):
        self[x] = self.load(x)
        return self[x]


def edges_kernel(X, s_h, c_h, a_h, b_h, own_h, buf, sem_in, sem_out):
    par = lax.rem(lax.axis_index("tile"), 2)
    picks = []
    for side in range(2):
        for n, (h, x) in enumerate(((s_h, 0), (c_h, 0), (c_h, 1), (c_h, 2))):
            x = x if side == 0 else X - 1 - x
            picks.append((side, n, copy(h.at[:, x // SUB, :, x % SUB], buf.at[side, n], sem_in.at[side, n])))
    for _, _, d in picks:
        d.start()
    for _, _, d in picks:
        d.wait()
    for side in range(2):
        copy(buf.at[side, 3], own_h.at[side], sem_out.at[side, 1]).start()

        @pl.when(par == 1 - side)
        def _():
            copy(buf.at[side, 0:3], a_h, sem_out.at[side, 0]).start()

        @pl.when(par == side)
        def _():
            copy(buf.at[side, 0:3], b_h, sem_out.at[side, 0]).start()

    for side in range(2):
        copy(buf.at[side, 3], own_h.at[side], sem_out.at[side, 1]).wait()
        copy(buf.at[side, 0:3], a_h, sem_out.at[side, 0]).wait()


def edges(state, coeff):
    Z, X, Y = state.shape
    J = Y // LANES

    def view(x):
        return nat(x).reshape(Z, X // SUB, J, SUB, 1, LANES)

    hbm = pl.BlockSpec(memory_space=pltpu.HBM)
    layer = (Z, J, 1, LANES)
    a, b, own = pl.pallas_call(
        partial(edges_kernel, X),
        out_shape=[jax.ShapeDtypeStruct((3,) + layer, f32)] * 2 + [jax.ShapeDtypeStruct((2,) + layer, f32)],
        in_specs=[hbm] * 2,
        out_specs=[hbm] * 3,
        scratch_shapes=[pltpu.VMEM((2, 4) + layer, f32), pltpu.SemaphoreType.DMA((2, 4)), pltpu.SemaphoreType.DMA((2, 2))],
        compiler_params=pltpu.CompilerParams(vmem_limit_bytes=60 * MIB),
        cost_estimate=pl.CostEstimate(flops=0, bytes_accessed=8 * MIB, transcendentals=0),
        name="edges",
    )(view(state), view(coeff))
    return a.reshape(3, Z * J, LANES), b.reshape(3, Z * J, LANES), own.reshape(2, Z * J, LANES)


def laps_kernel(Z, X, J, full, *refs):
    if full:
        s_h, c_h, t_h, b_h, u_h, f_h, S_h, x_h = refs[:8]
        refs = refs[8:]
    else:
        s_h, c_h, t_h, b_h, u_h, A_h, B_h = refs[:7]
        refs = refs[7:]
    s_n, c_n, t_n, g_n, sr, m, w, v, cr, kr, ak, Ak, sem_in, sem_out = refs[:14]
    refs = refs[14:]
    if full:
        f_n, S_n, x_n = refs
        rows = [range(X)] * 4
        rows0 = range(X)
    else:
        (e_n,) = refs
        rows = [[x for x in range(X) if x < d or x >= X - d] for d in (3, 2, 1)] + [[]]
        rows0 = [x for x in range(X) if x < 4 or x >= X - 4]
    PR = X * J
    CH = U * PR
    n = Z // U
    PP = 2 * J * X
    ins = ((s_h, s_n, 0), (c_h, c_n, CH), (t_h, t_n, CH))

    def cin(k):
        return [copy(h.at[pl.ds(k * CH, CH)], d.at[pl.ds(k * CH + o, CH)], sem_in.at[a, k]) for a, (h, d, o) in enumerate(ins)]

    def cout(k):
        return [copy(d.at[pl.ds(k * CH + CH, CH)], h.at[pl.ds(k * CH, CH)], sem_out.at[a, k]) for a, (h, d) in enumerate(((f_h, f_n), (S_h, S_n)))]

    ghosts = [
        copy(b_h, g_n.at[pl.ds(0, PR)], sem_in.at[3, 0]),
        copy(u_h, g_n.at[pl.ds(PR, PR)], sem_in.at[3, 1]),
        copy(u_h, s_n.at[pl.ds(Z * PR, PR)], sem_in.at[3, 2]),
    ]
    for d in ghosts:
        d.start()
    for k in range(n):
        for d in cin(k):
            d.start()
    for ref in (sr, m, w, v):
        clear_pads(ref, U * X, J)
    zero = jnp.zeros((J, LANES), f32)
    masks = lane_masks(J)
    for d in ghosts:
        d.wait()

    def at(p, x):
        return ((p + 1) % U) * PP + x * 2 * J + J

    def ld(ref, p, x):
        return ref[pl.ds(at(p, x), J), :]

    def put(ref, p, x, val):
        ref[pl.ds(at(p, x), J), :] = val

    def cat(p, x):
        return pl.ds((p % U) * PR + x * J, J)

    def around(ref, p, x, cur):
        total = ld(ref, p - 1, x) + ld(ref, p + 1, x)
        if x > 0:
            total = total + cur[x - 1]
        if x < X - 1:
            total = total + cur[x + 1]
        return total + beside(ref, at(p, x), cur[x], J, masks)

    for x in rows0:
        put(sr, -1, x, g_n[row_at(0, x, J), :])

    def group(ii, _):
        base = pl.multiple_of(ii * CH, CH)

        @pl.when(ii < n)
        def _():
            for d in cin(ii):
                d.wait()

        first = ii == 0
        last = ii == n

        def layer_at(side, layer, p):
            return pl.ds(pl.multiple_of(ii * (U * J), U * J) + ((side * 3 + layer) * (Z + 2 * U) + p + U) * J, J)

        for u in range(U):
            c1, c2, c3, c4 = [Lines(lambda x, r=r, p=p: ld(r, p, x)) for r, p in ((sr, u - 1), (m, u - 3), (w, u - 5), (v, u - 7))]
            s_at = base + u * PR
            c_at = base + (u - 1) * PR + CH
            f_at = base + (u - 3) * PR + CH
            S_at = base + (u - 7) * PR + CH
            for x in range(X):
                if x in rows0:
                    put(sr, u, x, s_n[row_at(s_at, x, J), :])
                if x in rows[3]:
                    p = u - 7
                    S_n[row_at(S_at, x, J), :] = Ak[cat(p, x), :] + around(v, p, x, c4)
                if x in rows[2]:
                    p = u - 5
                    adj = ak[cat(p, x), :] + around(w, p, x, c3)
                    if full:
                        val = cr[cat(p, x), :] * adj
                        if u == 5:
                            x_n[row_at(pl.multiple_of(jnp.where(first, 0, 2 * PR), PR), x, J), :] = val + c3[x]
                        if u == 4:
                            x_n[row_at(pl.multiple_of(jnp.where(last, PR, 2 * PR), PR), x, J), :] = val + c3[x]
                        if u == 4:
                            val = jnp.where(first, zero, val)
                        if u == 5:
                            val = jnp.where(last, zero, val)
                        put(v, p, x, val)
                        Ak[cat(p, x), :] = kr[cat(p, x), :] * adj
                    else:
                        e_n[layer_at(0 if x == 0 else 1, 2, p), :] = adj
                if x in rows[1]:
                    p = u - 3
                    c = cr[cat(p, x), :]
                    k = kr[cat(p, x), :]
                    fin = c2[x] * k + c * around(m, p, x, c2)
                    if full:
                        f_n[row_at(f_at, x, J), :] = fin
                    a = fin - t_n[row_at(f_at, x, J), :]
                    if not full and x in (0, X - 1):
                        e_n[layer_at(0 if x == 0 else 1, 1, p), :] = a
                    val = c * a
                    if u == 2:
                        val = jnp.where(first, zero, val)
                    if u == 3:
                        val = jnp.where(last, zero, val)
                    put(w, p, x, val)
                    ak[cat(p, x), :] = k * a
                if x in rows[0]:
                    p = u - 1
                    c = c_n[row_at(c_at, x, J), :]
                    k = 1.0 - 6.0 * c
                    val = c1[x] * k + c * around(sr, p, x, c1)
                    if u == 0:
                        val = jnp.where(first, g_n[row_at(0, x, J), :], val)
                    if u == 1:
                        val = jnp.where(last, g_n[row_at(PR, x, J), :], val)
                    if not full and x in (0, X - 1):
                        e_n[layer_at(0 if x == 0 else 1, 0, p), :] = val
                    put(m, p, x, val)
                    cr[cat(p, x), :] = c
                    kr[cat(p, x), :] = k
        if full:

            @pl.when(ii >= 1)
            def _():
                for d in cout(ii - 1):
                    d.start()

        return 0

    lax.fori_loop(0, n + 1, group, 0)
    if full:
        flux = copy(x_n.at[pl.ds(0, 2 * PR)], x_h, sem_out.at[2, 0])
        flux.start()
        for k in range(n):
            for d in cout(k):
                d.wait()
        flux.wait()
    else:
        par = lax.rem(lax.axis_index("tile"), 2)

        def out(side, layer, h):
            return copy(e_n.at[pl.ds(((side * 3 + layer) * (Z + 2 * U) + U) * J, Z * J)], h.at[layer], sem_out.at[side, layer])

        for side in range(2):

            @pl.when(par == 1 - side)
            def _():
                for layer in range(3):
                    out(side, layer, A_h).start()

            @pl.when(par == side)
            def _():
                for layer in range(3):
                    out(side, layer, B_h).start()

        for side in range(2):
            for layer in range(3):
                out(side, layer, A_h).wait()


def laps(full, state, coeff, target, below, above):
    Z, X, Y = state.shape
    J = Y // LANES
    N, PR = Z * X * J, X * J
    hbm = pl.BlockSpec(memory_space=pltpu.HBM)
    ring = pltpu.VMEM((U * X * 2 * J + J, LANES), f32)
    short = pltpu.VMEM((U * PR, LANES), f32)
    big = pltpu.VMEM((N + 2 * U * PR, LANES), f32)
    scratch = [big] * 3 + [pltpu.VMEM((2 * PR, LANES), f32)] + [ring] * 4 + [short] * 4
    scratch += [pltpu.SemaphoreType.DMA((4, max(Z // U, 3))), pltpu.SemaphoreType.DMA((3, max(Z // U, 3)))]
    if full:
        outs = [jax.ShapeDtypeStruct((N, LANES), f32)] * 2 + [jax.ShapeDtypeStruct((2 * PR, LANES), f32)]
        scratch += [big] * 2 + [pltpu.VMEM((3 * PR, LANES), f32)]
        specs = [pl.BlockSpec(memory_space=pl.ANY)] * 3
    else:
        outs = [jax.ShapeDtypeStruct((3, Z * J, LANES), f32)] * 2
        scratch += [pltpu.VMEM((6 * (Z + 2 * U) * J, LANES), f32)]
        specs = [hbm] * 2
    return pl.pallas_call(
        partial(laps_kernel, Z, X, J, full),
        out_shape=outs,
        in_specs=[hbm] * 5,
        out_specs=specs,
        scratch_shapes=scratch,
        compiler_params=pltpu.CompilerParams(vmem_limit_bytes=(36 if full else 60) * MIB),
        cost_estimate=pl.CostEstimate(flops=N * LANES * (56 if full else 12), bytes_accessed=N * LANES * 4 * (5 if full else 3), transcendentals=0),
        name="block" if full else "rims",
    )(nat(state), nat(coeff), nat(target), nat(below), nat(above))


def fix_kernel(Z, X, J, head, *refs):
    ao1, bo1, ar1, br1, ao2, bo2, ar2, br2, own_h, f_i, S_i, x_i = refs[:12]
    refs = refs[12:]
    if head:
        (l_h,) = refs[:1]
        refs = refs[1:]
    else:
        f_h, S_h, x_h = refs[:3]
        refs = refs[3:]
    lay, f_n, S_n, x_n, rings, sums, sem_l, sem_in, sem_out = refs
    PR = X * J
    CH = U * PR
    n = Z // U
    groups = 1 if head else n + 1
    ZL = U if head else Z
    LP = (Z + 2 * U) * J
    par = lax.rem(lax.axis_index("tile"), 2)
    sets = ((ao1, bo1, 0), (ar1, br1, 3), (ao2, bo2, 6), (ar2, br2, 9))

    def layer_copy(side, o, i, h):
        return copy(h.at[i, pl.ds(0, ZL * J)], lay.at[side, o + i, pl.ds(U * J, ZL * J)], sem_l.at[side, o + i])

    for side in range(2):

        @pl.when(par == 1 - side)
        def _():
            for a, b, o in sets:
                for i in range(3):
                    layer_copy(side, o, i, a).start()

        @pl.when(par == side)
        def _():
            for a, b, o in sets:
                for i in range(3):
                    layer_copy(side, o, i, b).start()

        copy(own_h.at[side, pl.ds(0, ZL * J)], lay.at[side, 12, pl.ds(U * J, ZL * J)], sem_l.at[side, 12]).start()

    def cin(k):
        return [copy(h.at[pl.ds(k * CH, CH)], d.at[pl.ds(k * CH + CH, CH)], sem_in.at[a, k]) for a, (h, d) in enumerate(((f_i, f_n), (S_i, S_n)))]

    def cout(k):
        return [copy(d.at[pl.ds(k * CH + CH, CH)], h.at[pl.ds(k * CH, CH)], sem_out.at[a, k]) for a, (h, d) in enumerate(((f_h, f_n), (S_h, S_n)))]

    flux = copy(x_i, x_n.at[pl.ds(0, 2 * PR)], sem_in.at[2, 0])
    flux.start()
    if head:
        plane = copy(f_i.at[pl.ds(0, PR)], f_n.at[pl.ds(CH, PR)], sem_in.at[0, 0])
        plane.start()
    else:
        for k in range(n):
            for d in cin(k):
                d.start()
    fields = 8
    for side in range(2):
        for q in range(fields):
            clear_pads(rings.at[side, q], U, J)
    zero = jnp.zeros((J, LANES), f32)
    masks = lane_masks(J)
    for side in range(2):
        for q in range(fields):
            rings[side, q, pl.ds(J, J), :] = zero
    for side in range(2):
        for i in range(13):
            copy(own_h.at[side, pl.ds(0, ZL * J)], lay.at[side, i, pl.ds(U * J, ZL * J)], sem_l.at[side, i]).wait()
    flux.wait()
    if head:
        plane.wait()

    def at(p):
        return ((p + 1) % U) * 2 * J + J

    def group(ii, _):
        base = pl.multiple_of(ii * CH, CH)
        lbase = pl.multiple_of(ii * (U * J), U * J)
        first = ii == 0
        last = ii == n
        if not head:

            @pl.when(ii < n)
            def _():
                for d in cin(ii):
                    d.wait()

        for u in range(U):
            for side in range(2):

                def layer(i, p):
                    return lay[side, i, pl.ds(lbase + (p + U) * J, J), :]

                def ld(q, p):
                    return rings[side, q, pl.ds(at(p), J), :]

                def put(q, p, val, lo, hi):
                    if p % U == U - 1 and lo:
                        val = jnp.where(first, zero, val)
                    if p % U == 0 and hi and not head:
                        val = jnp.where(last, zero, val)
                    rings[side, q, pl.ds(at(p), J), :] = val

                def keep(q, p, val):
                    sums[side, q, pl.ds((p % U) * J, J), :] = val

                def kept(q, p):
                    return sums[side, q, pl.ds((p % U) * J, J), :]

                def lat(q, p, centre):
                    ref = rings.at[side, q]
                    return ld(q, p - 1) + ld(q, p + 1) + beside(ref, at(p), centre, J, masks)

                def add(ref, p, depth, val):
                    x = depth if side == 0 else X - 1 - depth
                    where = row_at(base + p * PR + CH, x, J)
                    ref[where, :] = ref[where, :] + val

                p = u
                put(0, p, layer(1, p) * layer(3, p), False, True)
                put(1, p, layer(4, p) * layer(0, p), False, True)

                p = u - 2
                c0, cm1, c1, c2 = layer(1, p), layer(2, p), layer(4, p), layer(5, p)
                dm0, dm1 = ld(0, p), ld(1, p)
                m0, m1 = layer(6, p) + dm0, layer(9, p) + dm1
                df0 = dm0 - 6.0 * (c0 * dm0) + c0 * (lat(0, p, dm0) + m1)
                dfm = cm1 * dm0
                df1 = dm1 - 6.0 * (c1 * dm1) + c1 * (lat(1, p, dm1) + m0)
                if not head or p == 0:
                    add(f_n, p, 0, df0)
                    add(f_n, p, 1, dfm)
                dw0, dwm, dw1 = c0 * df0, cm1 * dfm, c1 * df1
                dw2 = c2 * (c2 * dm1)
                w1 = c1 * layer(10, p) + dw1
                w0 = c0 * layer(7, p) + dw0
                put(2, p, dw0, True, True)
                put(3, p, dwm, True, True)
                put(4, p, dw1, True, True)
                keep(0, p, df0 - 6.0 * dw0 + dwm + w1)
                keep(1, p, dfm - 6.0 * dwm + dw0)
                keep(2, p, df1 - 6.0 * dw1 + w0 + dw2 + layer(11, p))

                p = u - 4
                c0, cm1, c1, cm2 = layer(1, p), layer(2, p), layer(4, p), layer(12, p)
                dw0, dwm, dw1 = ld(2, p), ld(3, p), ld(4, p)
                dA0 = kept(0, p) + lat(2, p, dw0)
                dAm = kept(1, p) + lat(3, p, dwm)
                A1 = kept(2, p) + lat(4, p, dw1)
                dv0, dvm, dvn = c0 * dA0, cm1 * dAm, cm2 * dwm
                if (head and p == 0) or (not head and p % U == U - 1):
                    fl = 0 if head else pl.multiple_of(jnp.where(last, PR, 2 * PR), PR)
                    for depth, val in enumerate((dv0 + dw0, dvm + dwm, dvn)):
                        x = depth if side == 0 else X - 1 - depth
                        where = row_at(fl, x, J)
                        x_n[where, :] = x_n[where, :] + val
                if head:
                    continue
                put(5, p, dv0, True, True)
                put(6, p, dvm, True, True)
                put(7, p, dvn, True, True)
                keep(3, p, dA0 - 6.0 * dv0 + dvm + c1 * A1)
                keep(4, p, dAm - 6.0 * dvm + dv0 + dvn)
                keep(5, p, dwm - 6.0 * dvn + dvm)

                p = u - 6
                dv0, dvm, dvn = ld(5, p), ld(6, p), ld(7, p)
                add(S_n, p, 0, kept(3, p) + lat(5, p, dv0))
                add(S_n, p, 1, kept(4, p) + lat(6, p, dvm))
                add(S_n, p, 2, kept(5, p) + lat(7, p, dvn))
                add(S_n, p, 3, dvn)
        if not head:

            @pl.when(ii >= 1)
            def _():
                for d in cout(ii - 1):
                    d.start()

        return 0

    lax.fori_loop(0, groups, group, 0)
    if head:
        ends = [
            copy(f_n.at[pl.ds(CH, PR)], l_h.at[pl.ds(0, PR)], sem_out.at[0, 0]),
            copy(x_n.at[pl.ds(0, PR)], l_h.at[pl.ds(PR, PR)], sem_out.at[1, 0]),
        ]
        for d in ends:
            d.start()
        for d in ends:
            d.wait()
    else:
        end = copy(x_n.at[pl.ds(PR, PR)], x_h, sem_out.at[2, 0])
        end.start()
        for k in range(n):
            for d in cout(k):
                d.wait()
        end.wait()


def fix(head, shape, layers, f, S, flux):
    Z, X, Y = shape
    J = Y // LANES
    N, PR = Z * X * J, X * J
    anywhere = pl.BlockSpec(memory_space=pl.ANY)
    hbm = pl.BlockSpec(memory_space=pltpu.HBM)
    big = pltpu.VMEM((N + 2 * U * PR, LANES), f32)
    scratch = [
        pltpu.VMEM((2, 13, (Z + 2 * U) * J, LANES), f32),
        pltpu.VMEM((2 * U * PR, LANES), f32) if head else big,
        pltpu.VMEM((2 * U * PR, LANES), f32) if head else big,
        pltpu.VMEM((3 * PR, LANES), f32),
        pltpu.VMEM((2, 8, U * 2 * J + J, LANES), f32),
        pltpu.VMEM((2, 6, U * J, LANES), f32),
        pltpu.SemaphoreType.DMA((2, 13)),
        pltpu.SemaphoreType.DMA((3, Z // U)),
        pltpu.SemaphoreType.DMA((3, Z // U)),
    ]
    if head:
        outs = [jax.ShapeDtypeStruct((2 * PR, LANES), f32)]
    else:
        outs = [jax.ShapeDtypeStruct((N, LANES), f32)] * 2 + [jax.ShapeDtypeStruct((PR, LANES), f32)]
    return pl.pallas_call(
        partial(fix_kernel, Z, X, J, head),
        out_shape=outs,
        in_specs=[anywhere] * 12,
        out_specs=[hbm] * len(outs),
        scratch_shapes=scratch,
        compiler_params=pltpu.CompilerParams(vmem_limit_bytes=32 * MIB),
        cost_estimate=pl.CostEstimate(flops=N * LANES * (1 if head else 14), bytes_accessed=N * LANES * (1 if head else 16), transcendentals=0),
        name="head" if head else "fix",
    )(*layers, f, S, flux)


def swap_pairs(count, start):
    pairs = [(i, i + 1) for i in range(start, count - 1, 2)]
    return pairs + [(b, a) for a, b in pairs]


def shifted(block, axis, distance):
    devices = range(lax.axis_size(axis))
    route = [((i - distance) % len(devices), i) for i in devices]
    return lax.ppermute(block, axis, route)


def local(state, coeff, target, control, multiplier):
    shape = state.shape
    Z, X, Y = shape
    plane = control.shape
    count = lax.axis_size("tile")
    even, odd = swap_pairs(count, 0), swap_pairs(count, 1)

    below = shifted(control, "slab", 1)
    a1, b1, own = edges(state, coeff)
    a1r = lax.ppermute(a1, "tile", even)
    b1r = lax.ppermute(b1, "tile", odd)
    a2, b2 = laps(False, state, coeff, target, below, control)
    a2r = lax.ppermute(a2, "tile", even)
    b2r = lax.ppermute(b2, "tile", odd)
    f, S, flux = laps(True, state, coeff, target, below, control)
    layers = (a1, b1, a1r, b1r, a2, b2, a2r, b2r, own)
    (low,) = fix(True, shape, layers, f, S, flux)
    PR = X * (Y // LANES)
    low = shifted(low, "slab", -1)
    final, start, top = fix(False, shape, layers, f, S, flux)
    final, start = unnat(final, shape), unnat(start, shape)
    lower_trace, lower_flux = unnat(low[:PR], plane), unnat(low[PR:], plane)
    grad = unnat(top, plane) + lower_flux
    new_multiplier = multiplier + rho_step * (final[-1:] - lower_trace)
    new_control = (control - tau_step * (grad + new_multiplier)) / (1.0 + tau_step)
    return final, start, new_control, new_multiplier


def solution(mesh):
    spec = P("slab", "tile", None)
    return jax.shard_map(local, mesh=mesh, in_specs=(spec,) * 5, out_specs=(spec,) * 4, check_vma=False)
```

```python
from functools import partial

import jax
import jax.numpy as jnp
from jax import lax
from jax.experimental import pallas as pl
from jax.experimental.pallas import tpu as pltpu
from jax.sharding import PartitionSpec as P

rho_step = 0.5
tau_step = 0.5
f32 = jnp.float32
LANES = 128
SUB = 8
U = 8
MIB = 1 << 20


def copy(src, dst, sem):
    return pltpu.make_async_copy(src, dst, sem)


def nat(x):
    z, r, y = x.shape
    x = x.reshape(z, r // SUB, SUB, y // LANES, LANES).transpose(0, 1, 3, 2, 4)
    return x.reshape(z * r * y // LANES, LANES)


def unnat(x, shape):
    z, r, y = shape
    x = x.reshape(z, r // SUB, y // LANES, SUB, LANES).transpose(0, 1, 3, 2, 4)
    return x.reshape(shape)


def row_at(base, x, J):
    return pl.ds(base + (x // SUB) * (SUB * J) + x % SUB, J, stride=SUB)


def lane_masks(J):
    lane = lax.broadcasted_iota(jnp.int32, (J, LANES), 1)
    return lane == 0, lane == LANES - 1


def beside(ref, at, centre, J, masks):
    first, last = masks
    up = pltpu.roll(jnp.where(first, ref[pl.ds(at + 1, J), :], centre), LANES - 1, 1)
    down = pltpu.roll(jnp.where(last, ref[pl.ds(at - 1, J), :], centre), 1, 1)
    return up + down


def clear_pads(ref, lines, J):
    zero = jnp.zeros((J, LANES), f32)

    def body(i, _):
        for q in range(8):
            ref[pl.ds(pl.multiple_of(i * 16 * J, 16 * J) + q * 2 * J, J), :] = zero
        return 0

    lax.fori_loop(0, lines // 8, body, 0)
    ref[pl.ds(lines * 2 * J, J), :] = zero


class Lines(dict):
    def __init__(self, load):
        self.load = load

    def __missing__(self, x):
        self[x] = self.load(x)
        return self[x]


RAW = 9
WANT = ((0, 0), (1, 0), (1, 1), (1, 2), (0, 1), (0, 2), (0, 3), (2, 0), (2, 1))
LAYER = {("s", 0): 0, ("c", 0): 1, ("c", 1): 2, ("c", 2): 3, ("s", 1): 4, ("s", 2): 5, ("s", 3): 6, ("t", 0): 7, ("t", 1): 8}


def pick_kernel(X, s_h, c_h, t_h, a_v, b_v, own, sem_in, sem_out):
    par = lax.rem(lax.axis_index("tile"), 2)
    picks = []
    for i, (which, x) in enumerate(WANT):
        h = (s_h, c_h, t_h)[which]
        for side in range(2):
            r = x if side == 0 else X - 1 - x
            picks.append(copy(h.at[:, r // SUB, :, r % SUB], own.at[side * RAW + i], sem_in.at[side, i]))
    for d in picks:
        d.start()
    for d in picks[:6]:
        d.wait()
    for side in range(2):
        send = own.at[pl.ds(side * RAW, 3)]

        @pl.when(par == 1 - side)
        def _():
            copy(send, a_v, sem_out.at[side]).start()
            copy(send, a_v, sem_out.at[side]).wait()

        @pl.when(par == side)
        def _():
            copy(send, b_v, sem_out.at[side]).start()
            copy(send, b_v, sem_out.at[side]).wait()

    for d in picks[6:]:
        d.wait()


def in_hbm(x):
    return pltpu.with_memory_space_constraint(x, pltpu.HBM)


def in_vmem(x):
    return pltpu.with_memory_space_constraint(x, pltpu.VMEM)


HBM_SPEC = pl.BlockSpec(memory_space=pltpu.HBM)
VMEM_SPEC = pl.BlockSpec(memory_space=pltpu.VMEM)


def pick(state, coeff, target):
    Z, X, Y = state.shape
    J = Y // LANES

    def view(x):
        return in_hbm(nat(x).reshape(Z, X // SUB, J, SUB, 1, LANES))

    layer = (Z, J, 1, LANES)
    a, b, own = pl.pallas_call(
        partial(pick_kernel, X),
        out_shape=[pltpu.VMEM((3,) + layer, f32)] * 2 + [pltpu.VMEM((2 * RAW,) + layer, f32)],
        in_specs=[HBM_SPEC] * 3,
        out_specs=[VMEM_SPEC] * 3,
        scratch_shapes=[pltpu.SemaphoreType.DMA((2, RAW)), pltpu.SemaphoreType.DMA((2,))],
        compiler_params=pltpu.CompilerParams(vmem_limit_bytes=12 * MIB),
        cost_estimate=pl.CostEstimate(flops=0, bytes_accessed=8 * MIB, transcendentals=0),
        name="pick",
    )(view(state), view(coeff), view(target))
    return a.reshape(3 * Z * J, LANES), b.reshape(3 * Z * J, LANES), own.reshape(2 * RAW * Z * J, LANES)


def laps_kernel(Z, X, J, full, *refs):
    if full:
        b_v, u_v, s_h, c_h, t_h, f_v, S_v, x_v = refs[:8]
        refs = refs[8:]
        s_n, c_n, t_n, sr, m, w, v, cr, kr, ak, Ak, sem_in = refs
        rows = [range(X)] * 4
        rows0 = range(X)
        lag = (1, 3, 5, 7)
    else:
        b_v, u_v, own, a_h, b_h, e_v = refs[:6]
        refs = refs[6:]
        sr, m, w, v, cr, kr, ak, Ak, sem_out = refs
        rows = [[x for x in range(X) if x < d or x >= X - d] for d in (3, 2, 1)] + [[]]
        rows0 = [x for x in range(X) if x < 4 or x >= X - 4]
        lag = (1, 4, 7, 7)
    PR = X * J
    CH = U * PR
    n = Z // U
    PP = 2 * J * X

    if full:

        def cin(k):
            lo = pl.ds(k * CH, CH)
            return [copy(h.at[lo], d.at[lo], sem_in.at[a, k]) for a, (h, d) in enumerate(((s_h, s_n), (c_h, c_n), (t_h, t_n)))]

        for k in range(n):
            for d in cin(k):
                d.start()
    for ref in (sr, m, w, v):
        clear_pads(ref, U * X, J)
    zero = jnp.zeros((J, LANES), f32)
    masks = lane_masks(J)

    def at(p, x):
        return ((p + 1) % U) * PP + x * 2 * J + J

    def ld(ref, p, x):
        return ref[pl.ds(at(p, x), J), :]

    def put(ref, p, x, val):
        ref[pl.ds(at(p, x), J), :] = val

    def cat(p, x):
        return pl.ds((p % U) * PR + x * J, J)

    def around(ref, p, x, cur):
        total = ld(ref, p - 1, x) + ld(ref, p + 1, x)
        if x > 0:
            total = total + cur[x - 1]
        if x < X - 1:
            total = total + cur[x + 1]
        return total + beside(ref, at(p, x), cur[x], J, masks)

    for x in rows0:
        ghost = b_v[row_at(0, x, J), :]
        put(sr, -1, x, ghost)
        put(m, -1, x, ghost)
        put(w, -1, x, zero)
        put(v, -1, x, zero)

    def group(ii, kind):
        if kind == "mid":
            base = pl.multiple_of(ii * CH, CH)
            lbase = pl.multiple_of(ii * (U * J), U * J)
        else:
            base, lbase = ii * CH, ii * U * J
        if full and kind != "last":
            for d in cin(ii):
                d.wait()

        def raw(x, what, p):
            side, depth = (0, x) if x < X // 2 else (1, X - 1 - x)
            return own[pl.ds(lbase + ((side * RAW + LAYER[what, depth]) * Z + p) * J, J), :]

        def source(x, what, p):
            if full:
                ref = {"s": s_n, "c": c_n, "t": t_n}[what]
                return ref[row_at(base + p * PR, x, J), :]
            return raw(x, what, p)

        def rim(x, layer, p):
            side = 0 if x == 0 else 1
            return pl.ds(lbase + ((side * 3 + layer) * Z + p) * J, J)

        def live(p):
            return (kind != "first" or p >= 0) and (kind != "last" or p < 0)

        for u in range(U):
            planes = [u - d for d in lag]
            c1, c2, c3, c4 = [Lines(lambda x, r=r, p=p: ld(r, p, x)) for r, p in zip((sr, m, w, v), planes)]
            if kind == "last" and u == 0:
                for x in rows0:
                    ghost = u_v[row_at(0, x, J), :]
                    put(sr, 0, x, ghost)
                    put(m, 0, x, ghost)
            if kind == "last" and u == 2:
                for x in rows0:
                    put(w, 0, x, zero)
                    put(v, 0, x, zero)
            for x in range(X):
                if x in rows0 and kind != "last":
                    put(sr, u, x, source(x, "s", u))
                p = planes[3]
                if x in rows[3] and live(p):
                    S_v[row_at(base + p * PR, x, J), :] = Ak[cat(p, x), :] + around(v, p, x, c4)
                p = planes[2]
                if x in rows[2] and live(p):
                    adj = ak[cat(p, x), :] + around(w, p, x, c3)
                    if full:
                        val = cr[cat(p, x), :] * adj
                        if kind == "first" and p == 0:
                            x_v[row_at(0, x, J), :] = val + c3[x]
                        if kind == "last" and p == -1:
                            x_v[row_at(PR, x, J), :] = val + c3[x]
                        put(v, p, x, val)
                        Ak[cat(p, x), :] = kr[cat(p, x), :] * adj
                    else:
                        e_v[rim(x, 2, p), :] = adj
                p = planes[1]
                if x in rows[1] and live(p):
                    c = cr[cat(p, x), :]
                    k = kr[cat(p, x), :]
                    fin = c2[x] * k + c * around(m, p, x, c2)
                    if full:
                        f_v[row_at(base + p * PR, x, J), :] = fin
                    a = fin - source(x, "t", p)
                    if not full and x in (0, X - 1):
                        e_v[rim(x, 1, p), :] = a
                    put(w, p, x, c * a)
                    ak[cat(p, x), :] = k * a
                p = planes[0]
                if x in rows[0] and live(p):
                    c = source(x, "c", p)
                    k = 1.0 - 6.0 * c
                    val = c1[x] * k + c * around(sr, p, x, c1)
                    if not full and x in (0, X - 1):
                        e_v[rim(x, 0, p), :] = val
                    put(m, p, x, val)
                    cr[cat(p, x), :] = c
                    kr[cat(p, x), :] = k

    def middle(ii, _):
        group(ii, "mid")
        return 0

    group(0, "first")
    lax.fori_loop(1, n, middle, 0)
    group(n, "last")
    if not full:
        par = lax.rem(lax.axis_index("tile"), 2)

        def out(side, h):
            return copy(e_v.at[pl.ds(side * 3 * Z * J, 3 * Z * J)], h, sem_out.at[side])

        for side in range(2):

            @pl.when(par == 1 - side)
            def _():
                out(side, a_h).start()

            @pl.when(par == side)
            def _():
                out(side, b_h).start()

        for side in range(2):
            out(side, a_h).wait()


def laps_scratch(Z, X, J):
    ring = pltpu.VMEM((U * X * 2 * J + J, LANES), f32)
    short = pltpu.VMEM((U * X * J, LANES), f32)
    return [ring] * 4 + [short] * 4


def rims(own, below, above, shape):
    Z, X, Y = shape
    J = Y // LANES
    edge = (3 * Z * J, LANES)
    return pl.pallas_call(
        partial(laps_kernel, Z, X, J, False),
        out_shape=[jax.ShapeDtypeStruct(edge, f32)] * 2 + [pltpu.VMEM((2 * edge[0], LANES), f32)],
        in_specs=[VMEM_SPEC] * 3,
        out_specs=[HBM_SPEC] * 2 + [VMEM_SPEC],
        scratch_shapes=laps_scratch(Z, X, J) + [pltpu.SemaphoreType.DMA((2,))],
        compiler_params=pltpu.CompilerParams(vmem_limit_bytes=24 * MIB),
        cost_estimate=pl.CostEstimate(flops=12 * Z * X * Y, bytes_accessed=8 * MIB, transcendentals=0),
        name="rims",
    )(in_vmem(nat(below)), in_vmem(nat(above)), in_vmem(own))


def block(state, coeff, target, below, above):
    Z, X, Y = state.shape
    J = Y // LANES
    N, PR = Z * X * J, X * J
    scratch = [pltpu.VMEM((N, LANES), f32)] * 3 + laps_scratch(Z, X, J) + [pltpu.SemaphoreType.DMA((3, Z // U))]
    return pl.pallas_call(
        partial(laps_kernel, Z, X, J, True),
        out_shape=[pltpu.VMEM((N, LANES), f32)] * 2 + [pltpu.VMEM((2 * PR, LANES), f32)],
        in_specs=[VMEM_SPEC] * 2 + [HBM_SPEC] * 3,
        out_specs=[VMEM_SPEC] * 3,
        scratch_shapes=scratch,
        compiler_params=pltpu.CompilerParams(vmem_limit_bytes=36 * MIB),
        cost_estimate=pl.CostEstimate(flops=56 * N * LANES, bytes_accessed=20 * N * LANES, transcendentals=0),
        name="block",
    )(in_vmem(nat(below)), in_vmem(nat(above)), *[in_hbm(nat(x)) for x in (state, coeff, target)])


def fix_kernel(Z, X, J, head, *refs):
    own, rim, ar1, br1, ar2, br2, f_i, S_i, x_i = refs[:9]
    if head:
        l_v, rings, sums = refs[9:]
    else:
        _, f_v, S_v, f_h, S_h, x_v, rings, sums, sem_out = refs[9:]
    PR = X * J
    CH = U * PR
    n = Z // U
    par = lax.rem(lax.axis_index("tile"), 2)
    left = par == 0
    if head:
        l_v[pl.ds(0, PR), :] = f_i[pl.ds(0, PR), :]
        l_v[pl.ds(PR, PR), :] = x_i[pl.ds(0, PR), :]
    else:
        x_v[...] = x_i[pl.ds(PR, PR), :]
    fields = 8
    zero = jnp.zeros((J, LANES), f32)
    masks = lane_masks(J)
    for side in range(2):
        for q in range(fields):
            clear_pads(rings.at[side, q], U, J)
            rings[side, q, pl.ds(J, J), :] = zero

    def cout(k, a, lo=0, planes=U):
        h, d = ((f_h, f_v), (S_h, S_v))[a]
        where = pl.ds(k * CH + lo * PR, planes * PR)
        return copy(d.at[where], h.at[where], sem_out.at[a, k])

    def at(p):
        return ((p + 1) % U) * 2 * J + J

    def group(ii, kind):
        if kind == "mid":
            base = pl.multiple_of(ii * CH, CH)
            lbase = pl.multiple_of(ii * (U * J), U * J)
        else:
            base, lbase = ii * CH, ii * U * J

        def live(p):
            return (kind != "first" or p >= 0) and (kind != "last" or p < 0)

        for u in range(U):
            if not head and kind != "first" and u == 1:
                cout(ii - 1, 0).start()
            if kind == "last" and u in (0, 2):
                for side in range(2):
                    for q in range(fields):
                        if (q >= 5) == (u == 2):
                            rings[side, q, pl.ds(at(0), J), :] = zero
            for side in range(2):

                def mine(what, depth, p):
                    return own[pl.ds(lbase + ((side * RAW + LAYER[what, depth]) * Z + p) * J, J), :]

                def edge(i, p):
                    return rim[pl.ds(lbase + ((side * 3 + i) * Z + p) * J, J), :]

                def far(refs, i, p):
                    where = pl.ds(lbase + (i * Z + p) * J, J)
                    a, b = refs[0][where, :], refs[1][where, :]
                    return jnp.where(left, b, a) if side == 0 else jnp.where(left, a, b)

                raw, done = (ar1, br1), (ar2, br2)

                def ld(q, p):
                    return rings[side, q, pl.ds(at(p), J), :]

                def put(q, p, val):
                    rings[side, q, pl.ds(at(p), J), :] = val

                def keep(q, p, val):
                    sums[side, q, pl.ds((p % U) * J, J), :] = val

                def kept(q, p):
                    return sums[side, q, pl.ds((p % U) * J, J), :]

                def lat(q, p, centre):
                    return ld(q, p - 1) + ld(q, p + 1) + beside(rings.at[side, q], at(p), centre, J, masks)

                def add(ref, first, depth, val):
                    where = row_at(first, depth if side == 0 else X - 1 - depth, J)
                    ref[where, :] = ref[where, :] + val

                p = u
                if kind != "last" and not (head and p > 2):
                    put(0, p, mine("c", 0, p) * far(raw, 0, p))
                    put(1, p, far(raw, 1, p) * mine("s", 0, p))

                p = u - 1
                if live(p) and not (head and p > 1):
                    c0, cm1 = mine("c", 0, p), mine("c", 1, p)
                    c1, c2 = far(raw, 1, p), far(raw, 2, p)
                    dm0, dm1 = ld(0, p), ld(1, p)
                    m0, m1 = edge(0, p) + dm0, far(done, 0, p) + dm1
                    df0 = dm0 + c0 * (lat(0, p, dm0) + m1 - 6.0 * dm0)
                    dfm = cm1 * dm0
                    df1 = dm1 + c1 * (lat(1, p, dm1) + m0 - 6.0 * dm1)
                    if head:
                        if p == 0:
                            add(l_v, 0, 0, df0)
                            add(l_v, 0, 1, dfm)
                    else:
                        add(f_v, base + p * PR, 0, df0)
                        add(f_v, base + p * PR, 1, dfm)
                    dw0, dwm, dw1 = c0 * df0, cm1 * dfm, c1 * df1
                    dw2 = c2 * (c2 * dm1)
                    w1 = c1 * far(done, 1, p) + dw1
                    w0 = c0 * edge(1, p) + dw0
                    put(2, p, dw0)
                    put(3, p, dwm)
                    put(4, p, dw1)
                    keep(0, p, df0 - 6.0 * dw0 + (dwm + w1))
                    keep(1, p, dfm - 6.0 * dwm + dw0)
                    keep(2, p, df1 - 6.0 * dw1 + (w0 + dw2) + far(done, 2, p))

                p = u - 4
                if live(p) and not (head and p > 0):
                    c0, cm1, cm2 = mine("c", 0, p), mine("c", 1, p), mine("c", 2, p)
                    c1 = far(raw, 1, p)
                    dw0, dwm, dw1 = ld(2, p), ld(3, p), ld(4, p)
                    dA0 = kept(0, p) + lat(2, p, dw0)
                    dAm = kept(1, p) + lat(3, p, dwm)
                    A1 = kept(2, p) + lat(4, p, dw1)
                    dv0, dvm, dvn = c0 * dA0, cm1 * dAm, cm2 * dwm
                    if head or (kind == "last" and p == -1):
                        for depth, val in enumerate((dv0 + dw0, dvm + dwm, dvn)):
                            add(l_v if head else x_v, PR if head else 0, depth, val)
                    if not head:
                        put(5, p, dv0)
                        put(6, p, dvm)
                        put(7, p, dvn)
                        keep(3, p, dA0 - 6.0 * dv0 + (dvm + c1 * A1))
                        keep(4, p, dAm - 6.0 * dvm + (dv0 + dvn))
                        keep(5, p, dwm - 6.0 * dvn + dvm)

                p = u - 7
                if live(p) and not head:
                    dv0, dvm, dvn = ld(5, p), ld(6, p), ld(7, p)
                    add(S_v, base + p * PR, 0, kept(3, p) + lat(5, p, dv0))
                    add(S_v, base + p * PR, 1, kept(4, p) + lat(6, p, dvm))
                    add(S_v, base + p * PR, 2, kept(5, p) + lat(7, p, dvn))
                    add(S_v, base + p * PR, 3, dvn)
            if kind == "last" and u == 3:
                cout(ii - 1, 1, 0, U // 2).start()
        if kind == "mid":
            cout(ii - 1, 1).start()
        if kind == "last":
            cout(ii - 1, 1, U // 2, U // 2).start()

    def middle(ii, _):
        group(ii, "mid")
        return 0

    group(0, "first")
    if not head:
        lax.fori_loop(1, n, middle, 0)
        group(n, "last")
        for k in range(n):
            for a in range(2):
                cout(k, a).wait()


def fix(head, shape, layers, f, S, flux, after=None):
    Z, X, Y = shape
    J = Y // LANES
    N, PR = Z * X * J, X * J
    scratch = [
        pltpu.VMEM((2, 8, U * 2 * J + J, LANES), f32),
        pltpu.VMEM((2, 6, U * J, LANES), f32),
    ]
    args = [in_vmem(x) for x in (*layers, f, S, flux)]
    specs = [VMEM_SPEC] * len(args)
    if head:
        outs, out_specs, aliases = [pltpu.VMEM((2 * PR, LANES), f32)], [VMEM_SPEC], {}
    else:
        outs = [pltpu.VMEM((N, LANES), f32)] * 2 + [jax.ShapeDtypeStruct((N, LANES), f32)] * 2 + [pltpu.VMEM((PR, LANES), f32)]
        out_specs = [VMEM_SPEC] * 2 + [HBM_SPEC] * 2 + [VMEM_SPEC]
        aliases = {6: 0, 7: 1}
        args.append(after)
        specs.append(pl.BlockSpec(memory_space=pl.ANY))
        scratch.append(pltpu.SemaphoreType.DMA((2, Z // U)))
    return pl.pallas_call(
        partial(fix_kernel, Z, X, J, head),
        out_shape=outs,
        in_specs=specs,
        out_specs=out_specs,
        scratch_shapes=scratch,
        input_output_aliases=aliases,
        compiler_params=pltpu.CompilerParams(vmem_limit_bytes=16 * MIB),
        cost_estimate=pl.CostEstimate(flops=N * LANES * (1 if head else 14), bytes_accessed=N * LANES * (1 if head else 16), transcendentals=0),
        name="head" if head else "fix",
    )(*args)


def swap_pairs(count, start):
    pairs = [(i, i + 1) for i in range(start, count - 1, 2)]
    return pairs + [(b, a) for a, b in pairs]


def shifted(block, axis, distance):
    devices = range(lax.axis_size(axis))
    route = [((i - distance) % len(devices), i) for i in devices]
    return lax.ppermute(block, axis, route)


def local(state, coeff, target, control, multiplier):
    shape = state.shape
    Z, X, Y = shape
    plane = control.shape
    count = lax.axis_size("tile")
    even, odd = swap_pairs(count, 0), swap_pairs(count, 1)

    below = shifted(control, "slab", 1)
    a1, b1, own = pick(state, coeff, target)
    a1 = lax.ppermute(a1, "tile", even)
    b1 = lax.ppermute(b1, "tile", odd)
    a2, b2, rim = rims(own, below, control, shape)
    a2 = lax.ppermute(a2, "tile", even)
    b2 = lax.ppermute(b2, "tile", odd)
    f, S, flux = block(state, coeff, target, below, control)
    layers = (own, rim, a1, b1, a2, b2)
    (low,) = fix(True, shape, layers, f, S, flux)
    PR = X * (Y // LANES)
    lower = shifted(low, "slab", -1)
    _, _, final, start, top = fix(False, shape, layers, f, S, flux, low)
    final, start = unnat(final, shape), unnat(start, shape)
    lower_trace, lower_flux = unnat(lower[:PR], plane), unnat(lower[PR:], plane)
    grad = unnat(top, plane) + lower_flux
    new_multiplier = multiplier + rho_step * (final[-1:] - lower_trace)
    new_control = (control - tau_step * (grad + new_multiplier)) / (1.0 + tau_step)
    return final, start, new_control, new_multiplier


def solution(mesh):
    spec = P("slab", "tile", None)
    return jax.shard_map(local, mesh=mesh, in_specs=(spec,) * 5, out_specs=(spec,) * 4, check_vma=False)
```
